32 devices in a mesh: head: 4 (over y, x), ctx: 8 (over z, core).
Axes of the slice: x: 2, y: 2, z: 4, core: 2. Of those that a mesh axis runs over, the one named last changes fastest.
Arguments:
- mla_queries: bfloat16 [128, 128, 576], P('head'), may hold values from -4 to 4
- latent_cache: bfloat16 [32768, 576], P('ctx'), may hold values from -4 to 4
- normalizers: float32 [128, 128], P('head'), may hold values from 9 to 15
- query_positions: int32 [128], replicated, may hold values from 0 to 65535, as said below
- key_positions: int32 [32768], P('ctx'), may hold values from 0 to 65535, as said below
- index_queries: bfloat16 [64, 128, 128], P('head'), may hold values from -24 to 24
- index_keys: bfloat16 [32768, 128], P(('ctx', 'head')), may hold values from -24 to 24
- index_weights: bfloat16 [64, 128], P('head'), may hold values from -16 to 16
Outputs:
- grad_queries: float32 [64, 128, 128], P('head')
- grad_weights: float32 [64, 128], P('head')
- grad_keys: float32 [32768, 128], P(('ctx', 'head'))
The draws below stay inside these ranges and needn't reach their ends.
Inputs may be any that keep to these rules, and one draw needn't show every extreme that they name: `query_positions`: every query position is one the keys' positions could reach. `key_positions`: key positions rise strictly along the keys.
All inputs are finite; a program needn't handle non-finite values.
Results may differ from the reference program's by a relative error of at most 0.00115.
The reference program's roundings to bfloat16 on the way (of `pre_grad`) count: a program that leaves them out, or rounds other values in their place, can miss the bound.
Values may be sent and summed in bfloat16 or wider, within the bound.
A program may use at most 128 MiB of HBM per device.

```python
import math
import jax
import jax.numpy as jnp
from jax import lax

H = 128
D_LAT = 512
D_ROPE = 64
HI = 64
DI = 128
QUERIES = 128
KEYS = 32768


def indexer_parts(key):
    folded = jax.random.fold_in(key, 17)
    streams = jax.random.split(folded, 4)
    raw_keys = jax.random.normal(streams[0], (KEYS, DI), jnp.float32)
    queries = jax.random.normal(streams[1], (HI, QUERIES, DI), jnp.float32)
    weights = 3.0 * jax.random.normal(streams[2], (HI, QUERIES), jnp.float32)
    scales = jnp.exp(jax.random.uniform(streams[3], (KEYS, 1), jnp.float32, math.log(0.7), math.log(1.4)))
    index_rows = raw_keys * scales
    return (jnp.clip(index_rows, -24.0, 24.0), jnp.clip(queries, -24.0, 24.0), jnp.clip(weights, -16.0, 16.0))


def draw_index_keys(key, part):
    return indexer_parts(key)[0].astype(jnp.bfloat16)


def draw_index_queries(key, part):
    return indexer_parts(key)[1].astype(jnp.bfloat16)


def draw_index_weights(key, part):
    return indexer_parts(key)[2].astype(jnp.bfloat16)


def draw_query_positions(key, part):
    first_stream, second_stream = jax.random.split(jax.random.fold_in(key, 11))
    spread = jax.random.randint(first_stream, (QUERIES,), 0, 2 * KEYS)
    late = jax.random.randint(second_stream, (4,), KEYS, 2 * KEYS)
    spread = spread.at[QUERIES - 4:].set(late)
    spread = spread.at[0].set(0).at[QUERIES - 1].set(2 * KEYS - 1)
    return spread.astype(jnp.int32)


def draw_key_positions(key, part):
    extra = jax.random.randint(jax.random.fold_in(key, 13), (KEYS,), 0, 2)
    extra = extra.at[0].set(0).at[KEYS - 1].set(1)
    return (2 * jnp.arange(KEYS, dtype=jnp.int32) + extra).astype(jnp.int32)


def steps_of(own_key, dims, cuts, smallest, high):
    level, own = 1.0, jax.random.fold_in(own_key, 6)
    for dim, shards_of in cuts:
        draws = jnp.exp(jax.random.uniform(jax.random.fold_in(own, dim), (shards_of,), jnp.float32, smallest / len(cuts), high / len(cuts)))
        level = level * jnp.repeat(draws, dims[dim] // shards_of).reshape([-1 if axis == dim else 1 for axis in range(len(dims))])
    return level


def gaussian(rng, shape, width, bound, cuts=(), held_as=jnp.bfloat16):
    values = width * jax.random.normal(rng, shape, jnp.float32)
    if cuts:
        values = values * steps_of(rng, shape, cuts, -0.22, 0.18)
    return jnp.clip(values, -bound, bound).astype(held_as)


def setup_inputs(seed: int = 0) -> dict:
    key_list = jax.random.split(jax.random.key(seed), 9)
    mla_queries = gaussian(key_list[0], (H, QUERIES, D_LAT + D_ROPE), 1.0, 4.0, ((0, 4),))
    latent_cache = gaussian(key_list[1], (KEYS, D_LAT + D_ROPE), 1.0, 4.0, ((0, 8),))
    normalizers = jnp.clip(9.0 + 6.0 * jax.random.uniform(key_list[2], (H, QUERIES), jnp.float32) ** steps_of(key_list[2], (H, QUERIES), ((0, 4),), -0.2, 0.2), 9.0, 15.0)
    query_positions = draw_query_positions(jax.random.fold_in(key_list[8], 71), 0)
    key_positions = draw_key_positions(jax.random.fold_in(key_list[8], 71), 0)
    index_queries = draw_index_queries(jax.random.fold_in(key_list[8], 71), 0)
    index_keys = draw_index_keys(jax.random.fold_in(key_list[8], 71), 0)
    index_weights = draw_index_weights(jax.random.fold_in(key_list[8], 71), 0)
    return {"mla_queries": mla_queries, "latent_cache": latent_cache, "normalizers": normalizers, "query_positions": query_positions, "key_positions": key_positions, "index_queries": index_queries, "index_keys": index_keys, "index_weights": index_weights}


att_scale = 192.0 ** -0.5
loss_scale = 1024.0
masked_floor = -1.0e30


def reference(mla_queries, latent_cache, normalizers, query_positions, key_positions, index_queries, index_keys, index_weights):
    head_total = mla_queries.shape[0]
    query_count = mla_queries.shape[1]
    query_flat = mla_queries.reshape(head_total * query_count, mla_queries.shape[2])
    key_total = latent_cache.shape[0]
    block_rows = math.gcd(key_total, 1024)
    block_count = key_total // block_rows

    def probability_block(block_index):
        first_row = block_index * block_rows
        cache_rows = lax.dynamic_slice_in_dim(latent_cache, first_row, block_rows, 0)
        positions = lax.dynamic_slice_in_dim(key_positions, first_row, block_rows, 0)
        scores = jnp.dot(cache_rows, query_flat.T, preferred_element_type=jnp.float32)
        scores = scores.reshape(block_rows, head_total, query_count)
        weights = jnp.exp(scores * att_scale - normalizers[None])
        visible = positions[:, None] <= query_positions[None, :]
        return jnp.where(visible, jnp.sum(weights, axis=1), 0.0)

    block_ids = jnp.arange(block_count, dtype=jnp.int32)
    summed_probs = lax.map(probability_block, block_ids).reshape(key_total, query_count)

    index_heads = index_queries.shape[0]
    index_width = index_queries.shape[2]
    pair_flat = index_queries.reshape(index_heads * query_count, index_width)
    index_scale = (index_heads * index_width) ** -0.5
    weights_float = index_weights.astype(jnp.float32)

    def logit_block(block_index):
        first_row = block_index * block_rows
        key_rows = lax.dynamic_slice_in_dim(index_keys, first_row, block_rows, 0)
        relu_input = jnp.dot(key_rows, pair_flat.T, preferred_element_type=jnp.float32)
        relu_input = relu_input.reshape(block_rows, index_heads, query_count)
        return index_scale * jnp.sum(jnp.maximum(relu_input, 0.0) * weights_float[None], axis=1)

    logits = lax.map(logit_block, block_ids).reshape(key_total, query_count)
    visible_all = key_positions[:, None] <= query_positions[None, :]
    hidden_logits = jnp.where(visible_all, logits, masked_floor)
    row_max = jnp.max(hidden_logits, axis=0)
    exp_terms = jnp.where(visible_all, jnp.exp(hidden_logits - row_max[None]), 0.0)
    softmax_probs = exp_terms / jnp.sum(exp_terms, axis=0)[None]
    target = summed_probs / jnp.sum(summed_probs, axis=0)[None]
    logit_grad = loss_scale * jnp.where(visible_all, softmax_probs - target, 0.0)

    def gradient_block(carry, block_index):
        grad_query_sum, grad_weight_sum = carry
        first_row = block_index * block_rows
        key_rows = lax.dynamic_slice_in_dim(index_keys, first_row, block_rows, 0)
        grad_rows = lax.dynamic_slice_in_dim(logit_grad, first_row, block_rows, 0)
        relu_input = jnp.dot(key_rows, pair_flat.T, preferred_element_type=jnp.float32)
        relu_input = relu_input.reshape(block_rows, index_heads, query_count)
        gradient_gate = jnp.where(relu_input > 0.0, index_scale * weights_float[None], 0.0)
        pre_grad = (gradient_gate * grad_rows[:, None, :]).astype(jnp.bfloat16)
        pre_flat = pre_grad.reshape(block_rows, index_heads * query_count)
        query_term = jnp.dot(pre_flat.T, key_rows, preferred_element_type=jnp.float32)
        grad_query_sum = grad_query_sum + query_term.reshape(index_heads, query_count, index_width)
        grad_weight_sum = grad_weight_sum + jnp.sum(jnp.maximum(relu_input, 0.0) * grad_rows[:, None, :], axis=0)
        key_term = jnp.dot(pre_flat, pair_flat, preferred_element_type=jnp.float32)
        return (grad_query_sum, grad_weight_sum), key_term

    start_carry = (jnp.zeros((index_heads, query_count, index_width), jnp.float32), jnp.zeros((index_heads, query_count), jnp.float32))
    final_carry, key_blocks = lax.scan(gradient_block, start_carry, block_ids)
    grad_queries = final_carry[0]
    grad_weights = index_scale * final_carry[1]
    grad_keys = key_blocks.reshape(key_total, index_width)
    return (grad_queries, grad_weights, grad_keys)
```

```python
import functools
import math

import jax
import jax.numpy as jnp
from jax import lax
from jax.experimental import pallas as pl
from jax.experimental.pallas import tpu as pltpu
from jax.sharding import PartitionSpec as P

att_scale = 192.0 ** (-0.5)
loss_scale = 1024.0
masked_floor = -1e30
log2e = 1.4426950408889634
MESH = pl.DeviceIdType.MESH
NT = (((1,), (1,)), ((), ()))
NN = (((1,), (0,)), ((), ()))


def dot(a, b, dims):
    return lax.dot_general(a, b, dims, preferred_element_type=jnp.float32)


def kernel(
    q_ref, cache_ref, norm_ref, qpos_ref, kpos_ref, iq_ref, keys_ref, iw_ref,
    res_ref, gk_ref,
    part, rp, qs, ws, keys_t, lg, stat, stat_h, stat2, stat_c, pre,
    gbuf, pr, hs, hr, cs, zr, fin, res, nrm,
    s_part, r_part, s_q, r_q, s_w, r_w, s_sh, r_sh, s_sc, r_sc,
    s_pair, r_pair, s_head, r_head, s_z, r_z, s_ag, r_ag, s_fw, r_fw,
):
    n = lax.axis_size("head")
    nc = lax.axis_size("ctx")
    nz = nc // 2
    me = lax.axis_index("head")
    mc = lax.axis_index("ctx")
    par = lax.rem(mc, 2)
    z = lax.div(mc, 2)
    partner = z * 2 + (1 - par)
    sub, width = keys_ref.shape
    qn = qpos_ref.shape[1]
    hl = iw_ref.shape[0]
    mh = q_ref.shape[0] // qn
    nch = hl // nz
    nstep = nch * n
    iscale = (n * hl * width) ** (-0.5)

    def to_head(r):
        return {"head": lax.rem(me + r, n)}

    def head_copy(src, dst, ss, rs, r):
        return pltpu.make_async_remote_copy(
            src_ref=src, dst_ref=dst, send_sem=ss, recv_sem=rs,
            device_id=to_head(r), device_id_type=MESH)

    def ctx_copy(src, dst, ss, rs, c):
        return pltpu.make_async_remote_copy(
            src_ref=src, dst_ref=dst, send_sem=ss, recv_sem=rs,
            device_id={"ctx": c}, device_id_type=MESH)

    ws[0] = iw_ref[...].astype(jnp.float32)
    barrier = pltpu.get_barrier_semaphore()
    for r in range(1, n):
        pl.semaphore_signal(barrier, inc=1, device_id=to_head(r), device_id_type=MESH)
    for r in range(1, nc):
        pl.semaphore_signal(
            barrier, inc=1, device_id={"ctx": lax.rem(mc + r, nc)}, device_id_type=MESH)
    keys_t[...] = keys_ref[...].T
    qs[0] = iq_ref[...]
    nrm[...] = norm_ref[...] * log2e
    pl.semaphore_wait(barrier, n - 1 + nc - 1)

    q_copies = []
    for r in range(1, n):
        q_copies.append(head_copy(iq_ref, qs.at[r], s_q.at[r - 1], r_q.at[r - 1], r))
        q_copies.append(head_copy(ws.at[0], ws.at[r], s_w.at[r - 1], r_w.at[r - 1], r))
    for copy in q_copies:
        copy.start()

    rows = min(sub, 512)
    nblk = sub // rows
    hg = 4

    def part_copy(r, b):
        span = pl.ds(pl.multiple_of(b * rows, rows), rows)
        return head_copy(
            part.at[r, span], rp.at[r - 1, span],
            s_part.at[(r - 1) * nblk + b], r_part.at[(r - 1) * nblk + b], r)

    def mla_step(i, carry):
        r = lax.rem(lax.div(i, nblk) + 1, n)
        b = lax.rem(i, nblk)
        first = lax.rem(me + r, n) * sub + b * rows
        cache = cache_ref[pl.ds(pl.multiple_of(first, rows), rows), :]
        span = pl.ds(pl.multiple_of(b * rows, rows), rows)

        def group(g, acc_unused):
            qg = q_ref[pl.ds(pl.multiple_of(g * (hg * qn), hg * qn), hg * qn), :]
            x = dot(cache, qg, NT)
            total = None
            for h in range(hg):
                e = jnp.exp2(
                    x[:, h * qn:(h + 1) * qn] * (att_scale * log2e)
                    - nrm[pl.ds(g * hg + h, 1), :])
                total = e if total is None else total + e

            @pl.when(g == 0)
            def _():
                part[r, span, :] = total

            @pl.when(g > 0)
            def _():
                part[r, span, :] = part[r, span, :] + total

            return acc_unused

        lax.fori_loop(0, mh // hg, group, 0)

        @pl.when(r > 0)
        def _():
            part_copy(r, b).start()

        return carry

    lax.fori_loop(0, n * nblk, mla_step, 0)

    for copy in q_copies:
        copy.wait()
    lg[...] = jnp.zeros_like(lg)
    srows = min(sub, 256)
    ih = nz

    def logit_step(i, carry):
        r = lax.div(i, hl // ih)
        k = lax.rem(i, hl // ih)
        qg = qs[r, pl.ds(pl.multiple_of(k * (ih * qn), ih * qn), ih * qn), :]
        wg = ws[r, pl.ds(k * ih, ih), :]
        for sb in range(sub // srows):
            span = slice(sb * srows, (sb + 1) * srows)
            x = dot(keys_ref[span, :], qg, NT)
            total = lg[span, :]
            for h in range(ih):
                total = total + jnp.maximum(x[:, h * qn:(h + 1) * qn], 0.0) * wg[h:h + 1, :]
            lg[span, :] = total
        return carry

    lax.fori_loop(0, n * (hl // ih), logit_step, 0)

    for r in range(1, n):
        for b in range(nblk):
            part_copy(r, b).wait()
    visible = kpos_ref[...] <= qpos_ref[...]
    probs = part[0]
    for r in range(1, n):
        probs = probs + rp[r - 1]
    probs = jnp.where(visible, probs, 0.0)
    part[0] = probs
    hidden = jnp.where(visible, lg[...] * iscale, masked_floor)
    lg[...] = hidden
    local_max = jnp.max(hidden, axis=0, keepdims=True)
    local_sum = jnp.sum(
        jnp.where(visible, jnp.exp(hidden - local_max), 0.0), axis=0, keepdims=True)
    local_target = jnp.sum(probs, axis=0, keepdims=True)

    def exchange(own, mine, theirs, count, copy_of):
        mine[0:1, :] = own[0]
        mine[1:2, :] = own[1]
        mine[2:3, :] = own[2]
        mine[3:8, :] = jnp.zeros_like(mine[3:8, :])
        copies = [copy_of(r) for r in range(1, count)]
        for copy in copies:
            copy.start()
        for copy in copies:
            copy.wait()
        top = own[0]
        for r in range(1, count):
            top = jnp.maximum(top, theirs[r - 1, 0:1, :])
        total = own[1] * jnp.exp(own[0] - top)
        goal = own[2]
        for r in range(1, count):
            total = total + theirs[r - 1, 1:2, :] * jnp.exp(theirs[r - 1, 0:1, :] - top)
            goal = goal + theirs[r - 1, 2:3, :]
        return top, total, goal

    stats = exchange(
        (local_max, local_sum, local_target), stat, stat_h, n,
        lambda r: head_copy(stat, stat_h.at[r - 1], s_sh.at[r - 1], r_sh.at[r - 1], r))
    stats = exchange(
        stats, stat2, stat_c, nc,
        lambda r: ctx_copy(
            stat2, stat_c.at[r - 1], s_sc.at[r - 1], r_sc.at[r - 1], lax.rem(mc + r, nc)))
    row_max, row_total, target_total = stats
    soft = jnp.exp(lg[...] - row_max) * (1.0 / row_total)
    lg[...] = loss_scale * jnp.where(visible, soft - part[0] * (1.0 / target_total), 0.0)
    gk_ref[...] = jnp.zeros_like(gk_ref)

    half = width // 2
    tail = gbuf.shape[3] - half

    def pair_copy(i):
        return ctx_copy(gbuf.at[i, 1 - par], pr.at[i], s_pair.at[i], r_pair.at[i], partner)

    def head_send(i, k, r):
        return head_copy(hs.at[i], hr.at[k, r - 1], s_head.at[i], r_head.at[k * n + r], n - r)

    def z_copy(k, d):
        to = lax.rem(z + d, nz)
        at = k * nz + d
        return ctx_copy(cs.at[k, to], zr.at[k, d - 1], s_z.at[at], r_z.at[at], to * 2 + par)

    def ag_copy(k, d):
        to = lax.rem(z + d, nz)
        at = k * nz + d
        return ctx_copy(fin.at[k], res.at[0, k, d - 1], s_ag.at[at], r_ag.at[at], to * 2 + par)

    def fw_copy(k, d):
        at = k * nz + d
        src = fin.at[k] if d == 0 else res.at[0, k, d - 1]
        dst = res.at[1, k, nz - 1 if d == 0 else d - 1]
        return ctx_copy(src, dst, s_fw.at[at], r_fw.at[at], partner)

    def stage_pair(i):
        pair_copy(i).wait_recv()
        hs[i] = gbuf[i, par] + pr[i]
        k = lax.div(i, n)
        r = lax.rem(lax.rem(i, n) + 1, n)

        @pl.when(r > 0)
        def _():
            head_send(i, k, r).start()

    def stage_head(k):
        total = hs[k * n + n - 1]
        for r in range(1, n):
            head_send(k * n + r - 1, k, r).wait_recv()
            total = total + hr[k, r - 1]
        cs[k] = total
        for d in range(1, nz):
            z_copy(k, d).start()

    def stage_z(k):
        total = cs[k, z]
        for d in range(1, nz):
            z_copy(k, d).wait_recv()
            total = total + zr[k, d - 1]
        fin[k] = total
        for d in range(1, nz):
            ag_copy(k, d).start()
        fw_copy(k, 0).start()

    def stage_ag(k):
        for d in range(1, nz):
            ag_copy(k, d).wait_recv()
            fw_copy(k, d).start()

    def grad_step(i, carry):
        k = lax.div(i, n)
        r = lax.rem(lax.rem(i, n) + 1, n)
        qg = qs[r, pl.ds(pl.multiple_of(k * (nz * qn), nz * qn), nz * qn), :]
        wg = ws[r, pl.ds(k * nz, nz), :] * iscale
        sums = [[None] * nz, [None] * nz]
        nsb = sub // srows
        for sb in range(nsb):
            span = slice(sb * srows, (sb + 1) * srows)
            x = dot(keys_ref[span, :], qg, NT)
            grad = lg[span, :]
            side = sb * 2 // nsb
            for h in range(nz):
                xh = x[:, h * qn:(h + 1) * qn]
                gated = jnp.where(xh > 0.0, wg[h:h + 1, :] * grad, 0.0)
                pre[span, h * qn:(h + 1) * qn] = gated.astype(jnp.bfloat16)
                prod = jnp.maximum(xh, 0.0) * grad
                prod = jnp.sum(prod.reshape(srows // tail, tail, qn), axis=0)
                sums[side][h] = prod if sums[side][h] is None else sums[side][h] + prod
            gk_ref[span, :] += dot(pre[span, :], qg, NN)
        gq = dot(keys_t[...], pre[...], NN)
        for h in range(nz):
            for c in range(2):
                gbuf[i, c, h, 0:half, :] = gq[c * half:(c + 1) * half, h * qn:(h + 1) * qn]
                gbuf[i, c, h, half:half + tail, :] = sums[c][h]
        pair_copy(i).start()
        pl.when(i >= 1)(lambda: stage_pair(i - 1))
        at = lax.rem(i, n)
        pl.when((at == 2) & (i >= n))(lambda: stage_head(lax.div(i, n) - 1))
        pl.when((at == 0) & (i >= 2 * n))(lambda: stage_z(lax.div(i, n) - 2))
        pl.when((at == 2) & (i >= 2 * n))(lambda: stage_ag(lax.div(i, n) - 2))
        return carry

    lax.fori_loop(0, nstep, grad_step, 0)
    stage_pair(nstep - 1)
    head_done = max(nch - 1, 0)
    z_done = max(nch - 2, 0)
    for k in range(head_done, nch):
        stage_head(k)
    for k in range(z_done, nch):
        stage_z(k)
    for k in range(z_done, nch):
        stage_ag(k)

    for k in range(nch):
        for d in range(nz):
            fw_copy(k, d).wait_recv()
    for k in range(nch):
        res_ref[par, k, z] = fin[k]
        res_ref[1 - par, k, z] = res[1, k, nz - 1]
        for d in range(1, nz):
            src = lax.rem(z + nz - d, nz)
            res_ref[par, k, src] = res[0, k, d - 1]
            res_ref[1 - par, k, src] = res[1, k, d - 1]

    for i in range(nstep):
        pair_copy(i).wait_send()
        if (i % n + 1) % n:
            head_send(i, i // n, (i % n + 1) % n).wait_send()
    for k in range(nch):
        for d in range(1, nz):
            z_copy(k, d).wait_send()
            ag_copy(k, d).wait_send()
        for d in range(nz):
            fw_copy(k, d).wait_send()


def per_device(
    mla_queries, latent_cache, normalizers, query_positions, key_positions,
    index_queries, index_keys, index_weights,
):
    n = lax.axis_size("head")
    nc = lax.axis_size("ctx")
    nz = nc // 2
    mh, qn, lat = mla_queries.shape
    hl, _, width = index_queries.shape
    sub = index_keys.shape[0]
    nch = hl // nz
    nstep = nch * n
    rows = width // 2 + 8
    nblk = sub // min(sub, 512)
    own = lax.dynamic_slice_in_dim(
        key_positions, lax.axis_index("head") * sub, sub, 0)[:, None]
    f32 = jnp.float32
    dma = pltpu.SemaphoreType.DMA
    vm = pltpu.VMEM
    spec = pl.BlockSpec(memory_space=pltpu.VMEM)
    res, gk = pl.pallas_call(
        kernel,
        out_shape=(
            jax.ShapeDtypeStruct((2, nch, nz, rows, qn), f32),
            jax.ShapeDtypeStruct((sub, width), f32),
        ),
        in_specs=[spec] * 8,
        out_specs=(spec, spec),
        scratch_shapes=[
            vm((n, sub, qn), f32),
            vm((n - 1, sub, qn), f32),
            vm((n, hl * qn, width), jnp.bfloat16),
            vm((n, hl, qn), f32),
            vm((width, sub), jnp.bfloat16),
            vm((sub, qn), f32),
            vm((8, qn), f32),
            vm((n - 1, 8, qn), f32),
            vm((8, qn), f32),
            vm((nc - 1, 8, qn), f32),
            vm((sub, nz * qn), jnp.bfloat16),
            vm((nstep, 2, nz, rows, qn), f32),
            vm((nstep, nz, rows, qn), f32),
            vm((nstep, nz, rows, qn), f32),
            vm((nch, n - 1, nz, rows, qn), f32),
            vm((nch, nz, rows, qn), f32),
            vm((nch, nz - 1, rows, qn), f32),
            vm((nch, rows, qn), f32),
            vm((2, nch, nz, rows, qn), f32),
            vm((mh, qn), f32),
            dma(((n - 1) * nblk,)), dma(((n - 1) * nblk,)),
            dma((n - 1,)), dma((n - 1,)),
            dma((n - 1,)), dma((n - 1,)),
            dma((n - 1,)), dma((n - 1,)),
            dma((nc - 1,)), dma((nc - 1,)),
            dma((nstep,)), dma((nstep,)),
            dma((nstep,)), dma((nstep,)),
            dma((nch * nz,)), dma((nch * nz,)),
            dma((nch * nz,)), dma((nch * nz,)),
            dma((nch * nz,)), dma((nch * nz,)),
        ],
        compiler_params=pltpu.CompilerParams(
            collective_id=0, has_side_effects=True, vmem_limit_bytes=60 * 1024 * 1024),
    )(
        mla_queries.reshape(mh * qn, lat), latent_cache, normalizers,
        query_positions[None, :], own,
        index_queries.reshape(hl * qn, width), index_keys, index_weights,
    )
    half = width // 2
    body = res[:, :, :, :half, :].reshape(2, hl, half, qn)
    grad_queries = body.transpose(1, 3, 0, 2).reshape(hl, qn, width)
    scale = (n * hl * width) ** (-0.5)
    grad_weights = scale * jnp.sum(res[:, :, :, half:, :].reshape(2, hl, 8, qn), axis=(0, 2))
    return (grad_queries, grad_weights, gk)


def solution(mesh):
    placed = (
        P("head", None, None),
        P("ctx", None),
        P("head", None),
        P(),
        P("ctx"),
        P("head", None, None),
        P(("ctx", "head"), None),
        P("head", None),
    )
    return jax.shard_map(
        per_device,
        mesh=mesh,
        in_specs=placed,
        out_specs=(P("head", None, None), P("head", None), P(("ctx", "head"), None)),
        check_vma=False,
    )
```

```python
import functools
import math

import jax
import jax.numpy as jnp
from jax import lax
from jax.experimental import pallas as pl
from jax.experimental.pallas import tpu as pltpu
from jax.sharding import PartitionSpec as P

att_scale = 192.0 ** (-0.5)
loss_scale = 1024.0
masked_floor = -1e30
log2e = 1.4426950408889634
MESH = pl.DeviceIdType.MESH
NT = (((1,), (1,)), ((), ()))
NN = (((1,), (0,)), ((), ()))


def dot(a, b, dims):
    return lax.dot_general(a, b, dims, preferred_element_type=jnp.float32)


def kernel(
    q_hbm, cache_hbm, norm_ref, qpos_ref, kpos_ref, iq_ref, keys_ref, iw_ref,
    gq_ref, gw_ref, gk_ref,
    q_ref, cache_ref, ct, kp,
    part, rp, qs, ws, keys_t, lg, stat, stat_h, stat2, stat_c, pre,
    gbuf, pr, hs, hr, cs, zr, fin, res, nrm, l_q, l_c,
    s_part, r_part, s_q, r_q, s_qf, r_qf, s_w, r_w, s_sh, r_sh, s_sc, r_sc,
    s_pair, r_pair, s_head, r_head, s_z, r_z, s_ag, r_ag, s_fw, r_fw,
):
    n = lax.axis_size("head")
    nc = lax.axis_size("ctx")
    nz = nc // 2
    me = lax.axis_index("head")
    mc = lax.axis_index("ctx")
    par = lax.rem(mc, 2)
    z = lax.div(mc, 2)
    partner = z * 2 + (1 - par)
    sub, width = keys_ref.shape
    qn = qpos_ref.shape[1]
    hl = iw_ref.shape[0]
    mh = q_ref.shape[0]
    nch = hl // nz
    nstep = nch * n
    iscale = (n * hl * width) ** (-0.5)

    wide = 2 if n % 2 == 0 else 1
    deep = n // wide
    hi = lax.div(me, deep)
    lo = lax.rem(me, deep)

    def ahead(rh, rl):
        return lax.rem(hi + rh, wide) * deep + lax.rem(lo + rl, deep)

    def block_owner(r):
        return ahead(lax.div(r, deep), lax.rem(r, deep))

    def to_head(r):
        return {"head": lax.rem(me + r, n)}

    def head_copy(src, dst, ss, rs, head):
        return pltpu.make_async_remote_copy(
            src_ref=src, dst_ref=dst, send_sem=ss, recv_sem=rs,
            device_id={"head": head}, device_id_type=MESH)

    def hop(s, r):
        rh, rl = r // deep, r % deep
        first = rl > 0 if s == 0 else rh > 0
        if s == 0:
            return first, (ahead(0, rl) if first else ahead(rh, 0)), (rh * deep if first else 0)
        return first, (ahead(rh, 0) if first else ahead(0, rl)), (rl if first else 0)

    def ctx_copy(src, dst, ss, rs, c):
        return pltpu.make_async_remote_copy(
            src_ref=src, dst_ref=dst, send_sem=ss, recv_sem=rs,
            device_id={"ctx": c}, device_id_type=MESH)

    q_local = pltpu.make_async_copy(q_hbm, q_ref, l_q.at[0])
    q_local.start()

    def cache_copy(r):
        cols = pl.ds(pl.multiple_of(block_owner(r) * sub, 128), sub)
        return pltpu.make_async_copy(cache_hbm.at[:, cols], cache_ref.at[r], l_c.at[r])

    for r in reversed(range(n)):
        cache_copy(r).start()
    ws[0] = iw_ref[...].astype(jnp.float32)
    barrier = pltpu.get_barrier_semaphore()
    for r in range(1, n):
        pl.semaphore_signal(barrier, inc=1, device_id=to_head(r), device_id_type=MESH)
    for r in range(1, nc):
        pl.semaphore_signal(
            barrier, inc=1, device_id={"ctx": lax.rem(mc + r, nc)}, device_id_type=MESH)
    keys_t[...] = keys_ref[...].T
    qs[0] = iq_ref[...]
    nrm[...] = norm_ref[...] * log2e
    pl.semaphore_wait(barrier, n - 1 + nc - 1)

    qrows = hl * qn
    mine = pl.ds(pl.multiple_of(par * (qrows // 2), qrows // 2), qrows // 2)

    def q_copy(r):
        rh, rl = r // deep, r % deep
        return head_copy(
            iq_ref.at[mine], qs.at[r, mine], s_q.at[r - 1], r_q.at[r - 1],
            ahead(wide - rh, deep - rl))

    def w_copy(r):
        rh, rl = r // deep, r % deep
        return head_copy(
            ws.at[0], ws.at[r], s_w.at[r - 1], r_w.at[r - 1], ahead(wide - rh, deep - rl))

    def q_forward(r):
        return ctx_copy(
            qs.at[r, mine], qs.at[r, mine], s_qf.at[r - 1], r_qf.at[r - 1], partner)

    for r in range(1, n):
        q_copy(r).start()
        w_copy(r).start()

    rows = sub // 2
    hg = 4

    def part_copy(s, r):
        _, head, _ = hop(s, r)
        span = pl.ds(s * rows, rows)
        at = s * n + r
        return head_copy(
            part.at[r, span], rp.at[s, r - 1], s_part.at[at], r_part.at[at], head)

    def part_gather(s, r):
        span = slice(s * rows, (s + 1) * rows)
        total = part[r, span, :]
        for other in range(1, n):
            if other != r and hop(s, other)[2] == r:
                part_copy(s, other).wait_recv()
                total = total + rp[s, other - 1]
        part[r, span, :] = total

    def after_block(s, r):
        rh, rl = r // deep, r % deep
        if r and hop(s, r)[0]:
            part_copy(s, r).start()
        if s == 1 and rh == 0 and rl > 0:
            part_gather(1, rl)
            part_copy(1, rl).start()
            if rl == deep - 1:
                for outer in range(1, wide):
                    part_gather(0, outer * deep)
                    part_copy(0, outer * deep).start()
        if s == 0 and r == 0:
            for other in range(1, n):
                q_copy(other).wait_recv()
                q_forward(other).start()

    q_local.wait()

    def mla_step(i, carry):
        r = n - 1 - lax.div(i, 2)
        s = lax.rem(i, 2)
        span = pl.ds(pl.multiple_of(s * rows, rows), rows)

        @pl.when(s == 0)
        def _():
            cache_copy(r).wait()

        ct[...] = cache_ref[r, :, span].T

        def group(g, acc_unused):
            qg = jnp.concatenate([q_ref[g * hg + h] for h in range(hg)], axis=1)
            x = dot(ct[...], qg, NN)
            total = None
            for h in range(hg):
                e = jnp.exp2(
                    x[:, h * qn:(h + 1) * qn] * (att_scale * log2e)
                    - nrm[pl.ds(g * hg + h, 1), :])
                total = e if total is None else total + e

            @pl.when(g == 0)
            def _():
                part[r, span, :] = total

            @pl.when(g > 0)
            def _():
                part[r, span, :] = part[r, span, :] + total

            return acc_unused

        lax.fori_loop(0, mh // hg, group, 0)
        for j in range(2 * n):
            pl.when(i == j)(functools.partial(after_block, j % 2, n - 1 - j // 2))
        return carry

    lax.fori_loop(0, 2 * n, mla_step, 0)

    for r in range(1, n):
        q_copy(r).wait_send()
        w_copy(r).wait()
        q_forward(r).wait()
    lg[...] = jnp.zeros_like(lg)
    srows = min(sub, 256)
    ih = nz

    def logit_step(i, carry):
        r = lax.div(i, hl // ih)
        k = lax.rem(i, hl // ih)
        qg = qs[r, pl.ds(pl.multiple_of(k * (ih * qn), ih * qn), ih * qn), :]
        wg = ws[r, pl.ds(k * ih, ih), :]
        for sb in range(sub // srows):
            span = slice(sb * srows, (sb + 1) * srows)
            x = dot(keys_ref[span, :], qg, NT)
            total = lg[span, :]
            for h in range(ih):
                total = total + jnp.maximum(x[:, h * qn:(h + 1) * qn], 0.0) * wg[h:h + 1, :]
            lg[span, :] = total
        return carry

    lax.fori_loop(0, n * (hl // ih), logit_step, 0)

    for s in range(2):
        part_gather(s, 0)
    for block in range(sub // 128):
        kp[block * 128:(block + 1) * 128, :] = jnp.broadcast_to(
            kpos_ref[me, block:block + 1, :], (128, 128)).T
    visible = kp[:, 0:qn] <= qpos_ref[...]
    probs = part[0]
    probs = jnp.where(visible, probs, 0.0)
    part[0] = probs
    hidden = jnp.where(visible, lg[...] * iscale, masked_floor)
    lg[...] = hidden
    local_max = jnp.max(hidden, axis=0, keepdims=True)
    local_sum = jnp.sum(
        jnp.where(visible, jnp.exp(hidden - local_max), 0.0), axis=0, keepdims=True)
    local_target = jnp.sum(probs, axis=0, keepdims=True)

    def exchange(own, mine, theirs, count, copy_of):
        mine[0:1, :] = own[0]
        mine[1:2, :] = own[1]
        mine[2:3, :] = own[2]
        mine[3:8, :] = jnp.zeros_like(mine[3:8, :])
        copies = [copy_of(r) for r in range(1, count)]
        for copy in copies:
            copy.start()
        for copy in copies:
            copy.wait()
        top = own[0]
        for r in range(1, count):
            top = jnp.maximum(top, theirs[r - 1, 0:1, :])
        total = own[1] * jnp.exp(own[0] - top)
        goal = own[2]
        for r in range(1, count):
            total = total + theirs[r - 1, 1:2, :] * jnp.exp(theirs[r - 1, 0:1, :] - top)
            goal = goal + theirs[r - 1, 2:3, :]
        return top, total, goal

    stats = exchange(
        (local_max, local_sum, local_target), stat, stat_h, n,
        lambda r: head_copy(
            stat, stat_h.at[r - 1], s_sh.at[r - 1], r_sh.at[r - 1], lax.rem(me + r, n)))
    stats = exchange(
        stats, stat2, stat_c, nc,
        lambda r: ctx_copy(
            stat2, stat_c.at[r - 1], s_sc.at[r - 1], r_sc.at[r - 1], lax.rem(mc + r, nc)))
    row_max, row_total, target_total = stats
    soft = jnp.exp(lg[...] - row_max) * (1.0 / row_total)
    lg[...] = loss_scale * jnp.where(visible, soft - part[0] * (1.0 / target_total), 0.0)
    gk_ref[...] = jnp.zeros_like(gk_ref)

    half = width // 2
    tail = gbuf.shape[3] - half

    def pair_copy(i):
        return ctx_copy(gbuf.at[i, 1 - par], pr.at[i], s_pair.at[i], r_pair.at[i], partner)

    hhalf = nz // 2

    def head_send(k, s, r):
        _, head, _ = hop(s, r)
        span = pl.ds(s * hhalf, hhalf)
        at = (k * 2 + s) * n + r
        return head_copy(
            hs.at[k, r, span], hr.at[k, r - 1, span], s_head.at[at], r_head.at[at], head)

    def head_gather(k, s, r):
        span = slice(s * hhalf, (s + 1) * hhalf)
        total = hs[k, r, span]
        for other in range(1, n):
            if other != r and hop(s, other)[2] == r:
                head_send(k, s, other).wait_recv()
                total = total + hr[k, other - 1, span]
        return total

    def z_copy(k, d):
        to = lax.rem(z + d, nz)
        at = k * nz + d
        return ctx_copy(cs.at[k, to], zr.at[k, d - 1], s_z.at[at], r_z.at[at], to * 2 + par)

    def ag_copy(k, d):
        to = lax.rem(z + d, nz)
        at = k * nz + d
        return ctx_copy(fin.at[k], res.at[0, k, d - 1], s_ag.at[at], r_ag.at[at], to * 2 + par)

    def fw_copy(k, d):
        at = k * nz + d
        src = fin.at[k] if d == 0 else res.at[0, k, d - 1]
        dst = res.at[1, k, nz - 1 if d == 0 else d - 1]
        return ctx_copy(src, dst, s_fw.at[at], r_fw.at[at], partner)

    def stage_pair(i):
        pair_copy(i).wait_recv()
        k = lax.div(i, n)
        r = n - 1 - lax.rem(i, n)
        hs[k, r] = gbuf[i, par] + pr[i]
        for block in range(1, n):
            def send(block=block):
                for s in range(2):
                    if hop(s, block)[0]:
                        head_send(k, s, block).start()
            pl.when(r == block)(send)

    def stage_mid(k):
        for s in range(2):
            for r in range(1, n):
                if not hop(s, r)[0]:
                    hs[k, r, s * hhalf:(s + 1) * hhalf] = head_gather(k, s, r)
                    head_send(k, s, r).start()

    def stage_head(k):
        for s in range(2):
            cs[k, s * hhalf:(s + 1) * hhalf] = head_gather(k, s, 0)
        for d in range(1, nz):
            z_copy(k, d).start()

    def stage_z(k):
        total = cs[k, z]
        for d in range(1, nz):
            z_copy(k, d).wait_recv()
            total = total + zr[k, d - 1]
        fin[k] = total
        for d in range(1, nz):
            ag_copy(k, d).start()
        fw_copy(k, 0).start()

    def stage_ag(k):
        for d in range(1, nz):
            ag_copy(k, d).wait_recv()
            fw_copy(k, d).start()

    def grad_step(i, carry):
        k = lax.div(i, n)
        r = n - 1 - lax.rem(i, n)
        qg = qs[r, pl.ds(pl.multiple_of(k * (nz * qn), nz * qn), nz * qn), :]
        wg = ws[r, pl.ds(k * nz, nz), :] * iscale
        sums = [[None] * nz, [None] * nz]
        nsb = sub // srows
        for sb in range(nsb):
            span = slice(sb * srows, (sb + 1) * srows)
            x = dot(keys_ref[span, :], qg, NT)
            grad = lg[span, :]
            side = sb * 2 // nsb
            for h in range(nz):
                xh = x[:, h * qn:(h + 1) * qn]
                gated = jnp.where(xh > 0.0, wg[h:h + 1, :] * grad, 0.0)
                pre[span, h * qn:(h + 1) * qn] = gated.astype(jnp.bfloat16)
                prod = jnp.maximum(xh, 0.0) * grad
                prod = jnp.sum(prod.reshape(srows // tail, tail, qn), axis=0)
                sums[side][h] = prod if sums[side][h] is None else sums[side][h] + prod
            gk_ref[span, :] += dot(pre[span, :], qg, NN)
        gq = dot(keys_t[...], pre[...], NN)
        for h in range(nz):
            for c in range(2):
                gbuf[i, c, h, 0:half, :] = gq[c * half:(c + 1) * half, h * qn:(h + 1) * qn]
                gbuf[i, c, h, half:half + tail, :] = sums[c][h]
        pair_copy(i).start()
        pl.when(i >= 1)(lambda: stage_pair(i - 1))
        at = lax.rem(i, n)
        pl.when(at == n - 1)(lambda: stage_mid(lax.div(i, n)))
        pl.when((at == 2) & (i >= n))(lambda: stage_head(lax.div(i, n) - 1))
        pl.when((at == 0) & (i >= 2 * n))(lambda: stage_z(lax.div(i, n) - 2))
        pl.when((at == 2) & (i >= 2 * n))(lambda: stage_ag(lax.div(i, n) - 2))
        return carry

    lax.fori_loop(0, nstep, grad_step, 0)
    stage_pair(nstep - 1)
    head_done = max(nch - 1, 0)
    z_done = max(nch - 2, 0)
    for k in range(head_done, nch):
        stage_head(k)
    for k in range(z_done, nch):
        stage_z(k)
    for k in range(z_done, nch):
        stage_ag(k)

    for k in range(nch):
        for d in range(nz):
            fw_copy(k, d).wait_recv()
    for k in range(nch):
        res[0, k, nz - 1] = fin[k]
        for d in range(nz):
            slot = nz - 1 if d == 0 else d - 1
            head = k * nz + lax.rem(z + nz - d, nz)
            low = res[par, k, slot]
            high = res[1 - par, k, slot]
            gq_ref[head] = jnp.concatenate([low[:half], high[:half]], axis=0).T
            gw_ref[head] = iscale * jnp.sum(low[half:] + high[half:], axis=0, keepdims=True)

    for i in range(nstep):
        pair_copy(i).wait_send()
    for k in range(nch):
        for d in range(1, nz):
            z_copy(k, d).wait_send()
            ag_copy(k, d).wait_send()
        for d in range(nz):
            fw_copy(k, d).wait_send()
        for s in range(2):
            for r in range(1, n):
                head_send(k, s, r).wait_send()
    for s in range(2):
        for r in range(1, n):
            part_copy(s, r).wait_send()


def per_device(
    mla_queries, latent_cache, normalizers, query_positions, key_positions,
    index_queries, index_keys, index_weights,
):
    n = lax.axis_size("head")
    nc = lax.axis_size("ctx")
    nz = nc // 2
    mh, qn, lat = mla_queries.shape
    hl, _, width = index_queries.shape
    sub = index_keys.shape[0]
    nch = hl // nz
    nstep = nch * n
    rows = width // 2 + 8
    f32 = jnp.float32
    dma = pltpu.SemaphoreType.DMA
    vm = pltpu.VMEM
    spec = pl.BlockSpec(memory_space=pltpu.VMEM)
    hbm = pl.BlockSpec(memory_space=pl.ANY)
    gq, gw, gk = pl.pallas_call(
        kernel,
        out_shape=(
            jax.ShapeDtypeStruct((hl, qn, width), f32),
            jax.ShapeDtypeStruct((hl, 1, qn), f32),
            jax.ShapeDtypeStruct((sub, width), f32),
        ),
        in_specs=[hbm, hbm] + [spec] * 6,
        out_specs=(spec, spec, spec),
        scratch_shapes=[
            vm((mh, lat, qn), jnp.bfloat16),
            vm((n, lat, sub), jnp.bfloat16),
            vm((sub // 2, lat), jnp.bfloat16),
            vm((sub, 128), jnp.int32),
            vm((n, sub, qn), f32),
            vm((2, n - 1, sub // 2, qn), f32),
            vm((n, hl * qn, width), jnp.bfloat16),
            vm((n, hl, qn), f32),
            vm((width, sub), jnp.bfloat16),
            vm((sub, qn), f32),
            vm((8, qn), f32),
            vm((n - 1, 8, qn), f32),
            vm((8, qn), f32),
            vm((nc - 1, 8, qn), f32),
            vm((sub, nz * qn), jnp.bfloat16),
            vm((nstep, 2, nz, rows, qn), f32),
            vm((nstep, nz, rows, qn), f32),
            vm((nch, n, nz, rows, qn), f32),
            vm((nch, n - 1, nz, rows, qn), f32),
            vm((nch, nz, rows, qn), f32),
            vm((nch, nz - 1, rows, qn), f32),
            vm((nch, rows, qn), f32),
            vm((2, nch, nz, rows, qn), f32),
            vm((mh, qn), f32),
            dma((1,)), dma((n,)),
            dma((2 * n,)), dma((2 * n,)),
            dma((n - 1,)), dma((n - 1,)),
            dma((n - 1,)), dma((n - 1,)),
            dma((n - 1,)), dma((n - 1,)),
            dma((n - 1,)), dma((n - 1,)),
            dma((nc - 1,)), dma((nc - 1,)),
            dma((nstep,)), dma((nstep,)),
            dma((2 * nstep,)), dma((2 * nstep,)),
            dma((nch * nz,)), dma((nch * nz,)),
            dma((nch * nz,)), dma((nch * nz,)),
            dma((nch * nz,)), dma((nch * nz,)),
        ],
        compiler_params=pltpu.CompilerParams(
            collective_id=0, has_side_effects=True, vmem_limit_bytes=60 * 1024 * 1024),
    )(
        mla_queries.transpose(0, 2, 1), latent_cache.T, normalizers,
        query_positions[None, :], key_positions.reshape(n, sub // 128, 128),
        index_queries.reshape(hl * qn, width), index_keys, index_weights,
    )
    return (gq, gw.reshape(hl, qn), gk)


def solution(mesh):
    placed = (
        P("head", None, None),
        P("ctx", None),
        P("head", None),
        P(),
        P("ctx"),
        P("head", None, None),
        P(("ctx", "head"), None),
        P("head", None),
    )
    return jax.shard_map(
        per_device,
        mesh=mesh,
        in_specs=placed,
        out_specs=(P("head", None, None), P("head", None), P(("ctx", "head"), None)),
        check_vma=False,
    )
```

```python
import functools
import math

import jax
import jax.numpy as jnp
from jax import lax
from jax.experimental import pallas as pl
from jax.experimental.pallas import tpu as pltpu
from jax.sharding import PartitionSpec as P

att_scale = 192.0 ** (-0.5)
loss_scale = 1024.0
masked_floor = -1e30
log2e = 1.4426950408889634
MESH = pl.DeviceIdType.MESH
NT = (((1,), (1,)), ((), ()))
NN = (((1,), (0,)), ((), ()))


def dot(a, b, dims):
    return lax.dot_general(a, b, dims, preferred_element_type=jnp.float32)


def kernel(
    q_hbm, cache_hbm, norm_ref, qpos_ref, kpos_ref, iq_ref, keys_ref, iw_ref,
    gq_ref, gw_ref, gk_ref,
    q_ref, cache_ref, ct, kp,
    part, rp, qs, ws, keys_t, lg, stat, stat_h, stat2, stat_c, pre,
    gbuf, pr, hs, hr, cs, zr, fin, res, nrm, l_q, l_c,
    s_part, r_part, s_q, r_q, s_qf, r_qf, s_w, r_w, s_sh, r_sh, s_sc, r_sc,
    s_pair, r_pair, s_head, r_head, s_z, r_z, s_ag, r_ag, s_fw, r_fw,
):
    n = lax.axis_size("head")
    nc = lax.axis_size("ctx")
    nz = nc // 2
    me = lax.axis_index("head")
    mc = lax.axis_index("ctx")
    par = lax.rem(mc, 2)
    z = lax.div(mc, 2)
    partner = z * 2 + (1 - par)
    sub, width = keys_ref.shape
    qn = qpos_ref.shape[1]
    hl = iw_ref.shape[0]
    mh = q_ref.shape[0]
    nch = hl // nz
    nstep = nch * n
    iscale = (n * hl * width) ** (-0.5)

    wide = 2 if n % 2 == 0 else 1
    deep = n // wide
    hi = lax.div(me, deep)
    lo = lax.rem(me, deep)

    def ahead(rh, rl):
        return lax.rem(hi + rh, wide) * deep + lax.rem(lo + rl, deep)

    def block_owner(r):
        return ahead(lax.div(r, deep), lax.rem(r, deep))

    def to_head(r):
        return {"head": lax.rem(me + r, n)}

    def head_copy(src, dst, ss, rs, head):
        return pltpu.make_async_remote_copy(
            src_ref=src, dst_ref=dst, send_sem=ss, recv_sem=rs,
            device_id={"head": head}, device_id_type=MESH)

    def hop(s, r):
        rh, rl = r // deep, r % deep
        first = rl > 0 if s == 0 else rh > 0
        if s == 0:
            return first, (ahead(0, rl) if first else ahead(rh, 0)), (rh * deep if first else 0)
        return first, (ahead(rh, 0) if first else ahead(0, rl)), (rl if first else 0)

    def ctx_copy(src, dst, ss, rs, c):
        return pltpu.make_async_remote_copy(
            src_ref=src, dst_ref=dst, send_sem=ss, recv_sem=rs,
            device_id={"ctx": c}, device_id_type=MESH)

    q_local = pltpu.make_async_copy(q_hbm, q_ref, l_q.at[0])
    q_local.start()

    def cache_copy(r):
        cols = pl.ds(pl.multiple_of(block_owner(r) * sub, 128), sub)
        return pltpu.make_async_copy(cache_hbm.at[:, cols], cache_ref.at[r], l_c.at[r])

    for r in reversed(range(n)):
        cache_copy(r).start()
    ws[0] = iw_ref[...].astype(jnp.float32)
    barrier = pltpu.get_barrier_semaphore()
    for r in range(1, n):
        pl.semaphore_signal(barrier, inc=1, device_id=to_head(r), device_id_type=MESH)
    for r in range(1, nc):
        pl.semaphore_signal(
            barrier, inc=1, device_id={"ctx": lax.rem(mc + r, nc)}, device_id_type=MESH)
    keys_t[...] = keys_ref[...].T
    qs[0] = iq_ref[...]
    nrm[...] = norm_ref[...] * log2e
    pl.semaphore_wait(barrier, n - 1 + nc - 1)

    qrows = hl * qn
    mine = pl.ds(pl.multiple_of(par * (qrows // 2), qrows // 2), qrows // 2)

    def q_copy(r):
        rh, rl = r // deep, r % deep
        return head_copy(
            iq_ref.at[mine], qs.at[r, mine], s_q.at[r - 1], r_q.at[r - 1],
            ahead(wide - rh, deep - rl))

    def w_copy(r):
        rh, rl = r // deep, r % deep
        return head_copy(
            ws.at[0], ws.at[r], s_w.at[r - 1], r_w.at[r - 1], ahead(wide - rh, deep - rl))

    def q_forward(r):
        return ctx_copy(
            qs.at[r, mine], qs.at[r, mine], s_qf.at[r - 1], r_qf.at[r - 1], partner)

    for r in range(1, n):
        q_copy(r).start()
        w_copy(r).start()

    rows = sub // 2
    hg = 4
    mrows = min(rows, 256)

    def part_copy(s, r):
        _, head, _ = hop(s, r)
        span = pl.ds(s * rows, rows)
        at = s * n + r
        return head_copy(
            part.at[r, span], rp.at[s, r - 1], s_part.at[at], r_part.at[at], head)

    def part_gather(s, r):
        span = slice(s * rows, (s + 1) * rows)
        total = part[r, span, :]
        for other in range(1, n):
            if other != r and hop(s, other)[2] == r:
                part_copy(s, other).wait_recv()
                total = total + rp[s, other - 1]
        part[r, span, :] = total

    def after_block(s, r):
        rh, rl = r // deep, r % deep
        if r and hop(s, r)[0]:
            part_copy(s, r).start()
        if s == 1 and rh == 0 and rl > 0:
            part_gather(1, rl)
            part_copy(1, rl).start()
            if rl == deep - 1:
                for outer in range(1, wide):
                    part_gather(0, outer * deep)
                    part_copy(0, outer * deep).start()
        if s == 0 and r == 0:
            for other in range(1, n):
                q_copy(other).wait_recv()
                q_forward(other).start()

    q_local.wait()

    def mla_step(i, carry):
        r = n - 1 - lax.div(i, 2)
        s = lax.rem(i, 2)
        span = pl.ds(pl.multiple_of(s * rows, rows), rows)

        @pl.when(s == 0)
        def _():
            cache_copy(r).wait()

        ct[...] = cache_ref[r, :, span].T

        part[r, span, :] = jnp.zeros_like(part[r, span, :])

        def group(g, acc_unused):
            qg = jnp.concatenate([q_ref[g * hg + h] for h in range(hg)], axis=1)
            for sb in range(rows // mrows):
                piece = pl.ds(pl.multiple_of(s * rows + sb * mrows, mrows), mrows)
                x = dot(ct[sb * mrows:(sb + 1) * mrows, :], qg, NN)
                total = part[r, piece, :]
                for h in range(hg):
                    total = total + jnp.exp2(
                        x[:, h * qn:(h + 1) * qn] * (att_scale * log2e)
                        - nrm[pl.ds(g * hg + h, 1), :])
                part[r, piece, :] = total
            return acc_unused

        lax.fori_loop(0, mh // hg, group, 0, unroll=2)
        for j in range(2 * n):
            pl.when(i == j)(functools.partial(after_block, j % 2, n - 1 - j // 2))
        return carry

    lax.fori_loop(0, 2 * n, mla_step, 0)

    for r in range(1, n):
        q_copy(r).wait_send()
        w_copy(r).wait()
        q_forward(r).wait()
    lg[...] = jnp.zeros_like(lg)
    srows = min(sub, 256)
    ih = nz

    def logit_step(i, carry):
        r = lax.div(i, hl // ih)
        k = lax.rem(i, hl // ih)
        qg = qs[r, pl.ds(pl.multiple_of(k * (ih * qn), ih * qn), ih * qn), :]
        wg = ws[r, pl.ds(k * ih, ih), :]
        for sb in range(sub // srows):
            span = slice(sb * srows, (sb + 1) * srows)
            x = dot(keys_ref[span, :], qg, NT)
            total = lg[span, :]
            for h in range(ih):
                total = total + jnp.maximum(x[:, h * qn:(h + 1) * qn], 0.0) * wg[h:h + 1, :]
            lg[span, :] = total
        return carry

    lax.fori_loop(0, n * (hl // ih), logit_step, 0)

    for s in range(2):
        part_gather(s, 0)
    for block in range(sub // 128):
        kp[block * 128:(block + 1) * 128, :] = jnp.broadcast_to(
            kpos_ref[me, block:block + 1, :], (128, 128)).T
    visible = kp[:, 0:qn] <= qpos_ref[...]
    probs = part[0]
    probs = jnp.where(visible, probs, 0.0)
    part[0] = probs
    hidden = jnp.where(visible, lg[...] * iscale, masked_floor)
    lg[...] = hidden
    local_max = jnp.max(hidden, axis=0, keepdims=True)
    local_sum = jnp.sum(
        jnp.where(visible, jnp.exp(hidden - local_max), 0.0), axis=0, keepdims=True)
    local_target = jnp.sum(probs, axis=0, keepdims=True)

    def exchange(own, mine, theirs, count, copy_of):
        mine[0:1, :] = own[0]
        mine[1:2, :] = own[1]
        mine[2:3, :] = own[2]
        mine[3:8, :] = jnp.zeros_like(mine[3:8, :])
        copies = [copy_of(r) for r in range(1, count)]
        for copy in copies:
            copy.start()
        for copy in copies:
            copy.wait()
        top = own[0]
        for r in range(1, count):
            top = jnp.maximum(top, theirs[r - 1, 0:1, :])
        total = own[1] * jnp.exp(own[0] - top)
        goal = own[2]
        for r in range(1, count):
            total = total + theirs[r - 1, 1:2, :] * jnp.exp(theirs[r - 1, 0:1, :] - top)
            goal = goal + theirs[r - 1, 2:3, :]
        return top, total, goal

    stats = exchange(
        (local_max, local_sum, local_target), stat, stat_h, n,
        lambda r: head_copy(
            stat, stat_h.at[r - 1], s_sh.at[r - 1], r_sh.at[r - 1], lax.rem(me + r, n)))
    stats = exchange(
        stats, stat2, stat_c, nc,
        lambda r: ctx_copy(
            stat2, stat_c.at[r - 1], s_sc.at[r - 1], r_sc.at[r - 1], lax.rem(mc + r, nc)))
    row_max, row_total, target_total = stats
    soft = jnp.exp(lg[...] - row_max) * (1.0 / row_total)
    lg[...] = loss_scale * jnp.where(visible, soft - part[0] * (1.0 / target_total), 0.0)
    gk_ref[...] = jnp.zeros_like(gk_ref)

    half = width // 2
    tail = gbuf.shape[3] - half

    def pair_copy(i):
        return ctx_copy(gbuf.at[i, 1 - par], pr.at[i], s_pair.at[i], r_pair.at[i], partner)

    hhalf = nz // 2

    def head_send(k, s, r):
        _, head, _ = hop(s, r)
        span = pl.ds(s * hhalf, hhalf)
        at = (k * 2 + s) * n + r
        return head_copy(
            hs.at[k, r, span], hr.at[k, r - 1, span], s_head.at[at], r_head.at[at], head)

    def head_gather(k, s, r):
        span = slice(s * hhalf, (s + 1) * hhalf)
        total = hs[k, r, span]
        for other in range(1, n):
            if other != r and hop(s, other)[2] == r:
                head_send(k, s, other).wait_recv()
                total = total + hr[k, other - 1, span]
        return total

    def z_copy(k, d):
        to = lax.rem(z + d, nz)
        at = k * nz + d
        return ctx_copy(cs.at[k, to], zr.at[k, d - 1], s_z.at[at], r_z.at[at], to * 2 + par)

    def ag_copy(k, d):
        to = lax.rem(z + d, nz)
        at = k * nz + d
        return ctx_copy(fin.at[k], res.at[0, k, d - 1], s_ag.at[at], r_ag.at[at], to * 2 + par)

    def fw_copy(k, d):
        at = k * nz + d
        src = fin.at[k] if d == 0 else res.at[0, k, d - 1]
        dst = res.at[1, k, nz - 1 if d == 0 else d - 1]
        return ctx_copy(src, dst, s_fw.at[at], r_fw.at[at], partner)

    def stage_pair(i):
        pair_copy(i).wait_recv()
        k = lax.div(i, n)
        r = n - 1 - lax.rem(i, n)
        hs[k, r] = gbuf[i, par] + pr[i]
        for block in range(1, n):
            def send(block=block):
                for s in range(2):
                    if hop(s, block)[0]:
                        head_send(k, s, block).start()
            pl.when(r == block)(send)

    def stage_mid(k):
        for s in range(2):
            for r in range(1, n):
                if not hop(s, r)[0]:
                    hs[k, r, s * hhalf:(s + 1) * hhalf] = head_gather(k, s, r)
                    head_send(k, s, r).start()

    def stage_head(k):
        for s in range(2):
            cs[k, s * hhalf:(s + 1) * hhalf] = head_gather(k, s, 0)
        for d in range(1, nz):
            z_copy(k, d).start()

    def stage_z(k):
        total = cs[k, z]
        for d in range(1, nz):
            z_copy(k, d).wait_recv()
            total = total + zr[k, d - 1]
        fin[k] = total
        for d in range(1, nz):
            ag_copy(k, d).start()
        fw_copy(k, 0).start()

    def stage_ag(k):
        for d in range(1, nz):
            ag_copy(k, d).wait_recv()
            fw_copy(k, d).start()

    def grad_step(i, carry):
        k = lax.div(i, n)
        r = n - 1 - lax.rem(i, n)
        qg = qs[r, pl.ds(pl.multiple_of(k * (nz * qn), nz * qn), nz * qn), :]
        wg = ws[r, pl.ds(k * nz, nz), :] * iscale
        sums = [[None] * nz, [None] * nz]
        nsb = sub // srows
        for sb in range(nsb):
            span = slice(sb * srows, (sb + 1) * srows)
            x = dot(keys_ref[span, :], qg, NT)
            grad = lg[span, :]
            side = sb * 2 // nsb
            for h in range(nz):
                xh = x[:, h * qn:(h + 1) * qn]
                gated = jnp.where(xh > 0.0, wg[h:h + 1, :] * grad, 0.0)
                pre[span, h * qn:(h + 1) * qn] = gated.astype(jnp.bfloat16)
                prod = jnp.maximum(xh, 0.0) * grad
                prod = jnp.sum(prod.reshape(srows // tail, tail, qn), axis=0)
                sums[side][h] = prod if sums[side][h] is None else sums[side][h] + prod
            gk_ref[span, :] += dot(pre[span, :], qg, NN)
        gq = dot(keys_t[...], pre[...], NN)
        for h in range(nz):
            for c in range(2):
                gbuf[i, c, h, 0:half, :] = gq[c * half:(c + 1) * half, h * qn:(h + 1) * qn]
                gbuf[i, c, h, half:half + tail, :] = sums[c][h]
        pair_copy(i).start()
        pl.when(i >= 1)(lambda: stage_pair(i - 1))
        at = lax.rem(i, n)
        pl.when(at == n - 1)(lambda: stage_mid(lax.div(i, n)))
        pl.when((at == 2) & (i >= n))(lambda: stage_head(lax.div(i, n) - 1))
        pl.when((at == 0) & (i >= 2 * n))(lambda: stage_z(lax.div(i, n) - 2))
        pl.when((at == 2) & (i >= 2 * n))(lambda: stage_ag(lax.div(i, n) - 2))
        return carry

    lax.fori_loop(0, nstep, grad_step, 0)
    stage_pair(nstep - 1)
    head_done = max(nch - 1, 0)
    z_done = max(nch - 2, 0)
    for k in range(head_done, nch):
        stage_head(k)
    for k in range(z_done, nch):
        stage_z(k)
    for k in range(z_done, nch):
        stage_ag(k)

    for k in range(nch):
        for d in range(nz):
            fw_copy(k, d).wait_recv()
    for k in range(nch):
        res[0, k, nz - 1] = fin[k]
        for d in range(nz):
            slot = nz - 1 if d == 0 else d - 1
            head = k * nz + lax.rem(z + nz - d, nz)
            low = res[par, k, slot]
            high = res[1 - par, k, slot]
            gq_ref[head] = jnp.concatenate([low[:half], high[:half]], axis=0).T
            gw_ref[head] = iscale * jnp.sum(low[half:] + high[half:], axis=0, keepdims=True)

    for i in range(nstep):
        pair_copy(i).wait_send()
    for k in range(nch):
        for d in range(1, nz):
            z_copy(k, d).wait_send()
            ag_copy(k, d).wait_send()
        for d in range(nz):
            fw_copy(k, d).wait_send()
        for s in range(2):
            for r in range(1, n):
                head_send(k, s, r).wait_send()
    for s in range(2):
        for r in range(1, n):
            part_copy(s, r).wait_send()


def per_device(
    mla_queries, latent_cache, normalizers, query_positions, key_positions,
    index_queries, index_keys, index_weights,
):
    n = lax.axis_size("head")
    nc = lax.axis_size("ctx")
    nz = nc // 2
    mh, qn, lat = mla_queries.shape
    hl, _, width = index_queries.shape
    sub = index_keys.shape[0]
    nch = hl // nz
    nstep = nch * n
    rows = width // 2 + 8
    f32 = jnp.float32
    dma = pltpu.SemaphoreType.DMA
    vm = pltpu.VMEM
    spec = pl.BlockSpec(memory_space=pltpu.VMEM)
    hbm = pl.BlockSpec(memory_space=pl.ANY)
    gq, gw, gk = pl.pallas_call(
        kernel,
        out_shape=(
            jax.ShapeDtypeStruct((hl, qn, width), f32),
            jax.ShapeDtypeStruct((hl, 1, qn), f32),
            jax.ShapeDtypeStruct((sub, width), f32),
        ),
        in_specs=[hbm, hbm] + [spec] * 6,
        out_specs=(spec, spec, spec),
        scratch_shapes=[
            vm((mh, lat, qn), jnp.bfloat16),
            vm((n, lat, sub), jnp.bfloat16),
            vm((sub // 2, lat), jnp.bfloat16),
            vm((sub, 128), jnp.int32),
            vm((n, sub, qn), f32),
            vm((2, n - 1, sub // 2, qn), f32),
            vm((n, hl * qn, width), jnp.bfloat16),
            vm((n, hl, qn), f32),
            vm((width, sub), jnp.bfloat16),
            vm((sub, qn), f32),
            vm((8, qn), f32),
            vm((n - 1, 8, qn), f32),
            vm((8, qn), f32),
            vm((nc - 1, 8, qn), f32),
            vm((sub, nz * qn), jnp.bfloat16),
            vm((nstep, 2, nz, rows, qn), f32),
            vm((nstep, nz, rows, qn), f32),
            vm((nch, n, nz, rows, qn), f32),
            vm((nch, n - 1, nz, rows, qn), f32),
            vm((nch, nz, rows, qn), f32),
            vm((nch, nz - 1, rows, qn), f32),
            vm((nch, rows, qn), f32),
            vm((2, nch, nz, rows, qn), f32),
            vm((mh, qn), f32),
            dma((1,)), dma((n,)),
            dma((2 * n,)), dma((2 * n,)),
            dma((n - 1,)), dma((n - 1,)),
            dma((n - 1,)), dma((n - 1,)),
            dma((n - 1,)), dma((n - 1,)),
            dma((n - 1,)), dma((n - 1,)),
            dma((nc - 1,)), dma((nc - 1,)),
            dma((nstep,)), dma((nstep,)),
            dma((2 * nstep,)), dma((2 * nstep,)),
            dma((nch * nz,)), dma((nch * nz,)),
            dma((nch * nz,)), dma((nch * nz,)),
            dma((nch * nz,)), dma((nch * nz,)),
        ],
        compiler_params=pltpu.CompilerParams(
            collective_id=0, has_side_effects=True, vmem_limit_bytes=60 * 1024 * 1024),
    )(
        mla_queries.transpose(0, 2, 1), latent_cache.T, normalizers,
        query_positions[None, :], key_positions.reshape(n, sub // 128, 128),
        index_queries.reshape(hl * qn, width), index_keys, index_weights,
    )
    return (gq, gw.reshape(hl, qn), gk)


def solution(mesh):
    placed = (
        P("head", None, None),
        P("ctx", None),
        P("head", None),
        P(),
        P("ctx"),
        P("head", None, None),
        P(("ctx", "head"), None),
        P("head", None),
    )
    return jax.shard_map(
        per_device,
        mesh=mesh,
        in_specs=placed,
        out_specs=(P("head", None, None), P("head", None), P(("ctx", "head"), None)),
        check_vma=False,
    )
```
